512 devices in a mesh: cb: 16 (over z_lo, core), frame: 32 (over x, y, z_hi).
Axes of the slice: x: 4, y: 4, z: 16 (z_hi: 2, z_lo: 8; z = z_hi * 8 + z_lo), core: 2. Of those that a mesh axis runs over, the one named last changes fastest.
Arguments:
- inputs: bfloat16 [8192, 16, 1024], P('frame', 'cb'), may hold values from -64 to 64
- norm_gain: float32 [1024], replicated, may hold values from 0.1 to 1.9
- w_qkv: bfloat16 [16, 1024, 3072], P('cb', 'frame'), may hold values from -4 to 4
- w_out: bfloat16 [16, 1024, 1024], P('cb', 'frame'), may hold values from -0.1875 to 0.1875
- grad_out: bfloat16 [8192, 16, 1024], P('frame', 'cb'), may hold values from -6 to 6
Outputs:
- outputs: bfloat16 [8192, 16, 1024], P('frame', 'cb')
- grad_in: bfloat16 [8192, 16, 1024], P('frame', 'cb')
The draws below stay inside these ranges and needn't reach their ends.
All inputs are finite; a program needn't handle non-finite values.
Results may differ from the reference program's by a relative error of at most 0.0053.
Values may be sent and summed in bfloat16 or wider, within the bound.
A program may use at most 64 MiB of HBM per device.

```python
import math
import jax
import jax.numpy as jnp
from jax import lax

D = 1024
HEADS = 16
CODEBOOKS = 16
FR_DEV = 256
FRAMES = 8192


def draw_inputs(key, part):
    key_noise, key_rows, key_cols = jax.random.split(key, 3)
    shape_full = (FRAMES, CODEBOOKS, D)
    noise = jax.random.truncated_normal(key_noise, -4.0, 4.0, shape_full, jnp.float32)
    low = math.log(0.4)
    high = math.log(4.0)
    row_scale = jnp.exp(jax.random.uniform(key_rows, (FRAMES, CODEBOOKS, 1), jnp.float32, low, high))
    col_scale = jnp.exp(jax.random.uniform(key_cols, (1, 1, D), jnp.float32, low, high))
    return (noise * row_scale * col_scale).astype(jnp.bfloat16)


def draw_w_qkv(key, part):
    key_base = jax.random.fold_in(jax.random.fold_in(key, 7), 0)
    base = jax.random.truncated_normal(key_base, -4.0, 4.0, (CODEBOOKS, D, 3 * D), jnp.float32) / math.sqrt(D)
    return base.astype(jnp.bfloat16)


def block_scale(rng, extent, cuts, smallest, top_value):
    loudness = 1.0
    for dim, blocks in cuts:
        draws = jax.random.uniform(jax.random.fold_in(jax.random.fold_in(rng, 6), dim), (blocks,), jnp.float32, smallest / len(cuts), top_value / len(cuts))
        loudness = loudness * jnp.repeat(jnp.exp(draws), extent[dim] // blocks).reshape((-1,) + (1,) * (len(extent) - 1 - dim))
    return loudness


def gaussian(key, extent, scale, limit, cuts=(), dtype=jnp.bfloat16):
    entries = scale * jax.random.normal(key, extent, jnp.float32)
    if cuts:
        entries = entries * block_scale(key, extent, cuts, -0.22, 0.18)
    return jnp.clip(entries, -limit, limit).astype(dtype)


def setup_inputs(seed: int = 0) -> dict:
    arg_keys = jax.random.split(jax.random.key(seed), 6)
    return {
        "inputs": draw_inputs(jax.random.fold_in(arg_keys[5], 71), 0),
        "norm_gain": jnp.clip(1.0 + 0.18 * jax.random.normal(arg_keys[1], (D,), jnp.float32), 0.1, 1.9),
        "w_qkv": draw_w_qkv(jax.random.fold_in(arg_keys[5], 71), 0),
        "w_out": gaussian(arg_keys[3], (CODEBOOKS, D, D), D ** -0.5, 0.1875, ((0, 16), (1, 32))),
        "grad_out": gaussian(arg_keys[4], (FRAMES, CODEBOOKS, D), 1.0, 6.0, ((0, 32), (1, 16))),
    }


epsilon = 1e-05
highest = lax.Precision.HIGHEST

def rounded(values):
    return lax.optimization_barrier(values.astype(jnp.bfloat16))

def per_codebook(operand, weight):
    return jnp.einsum('fcd,cde->fce', operand.astype(jnp.float32), weight, precision=highest)

def per_codebook_back(operand, weight):
    return jnp.einsum('fce,cde->fcd', operand.astype(jnp.float32), weight, precision=highest)

def to_heads(values, head_count):
    frames, depth, columns = values.shape
    return values.reshape(frames, depth, head_count, columns // head_count).astype(jnp.float32)

def attention_probs(queries, key_rows, head_count):
    depth = queries.shape[1]
    factor = (queries.shape[2] // head_count) ** (-0.5)
    scores = jnp.einsum('fihe,fjhe->fhij', to_heads(queries, head_count), to_heads(key_rows, head_count), precision=highest) * factor
    causal = lax.broadcasted_iota(jnp.int32, (depth, depth), 0) >= lax.broadcasted_iota(jnp.int32, (depth, depth), 1)
    scores = jnp.where(causal, scores, -jnp.inf)
    weights = jnp.exp(scores - lax.optimization_barrier(jnp.max(scores, axis=-1, keepdims=True)))
    return weights / lax.optimization_barrier(jnp.sum(weights, axis=-1, keepdims=True))

def attention_grads(queries, key_rows, values, grad_context, head_count):
    shape_full = queries.shape
    factor = (queries.shape[2] // head_count) ** (-0.5)
    probs = attention_probs(queries, key_rows, head_count)
    probs_low = rounded(probs).astype(jnp.float32)
    grad_heads = to_heads(grad_context, head_count)
    grad_values = jnp.einsum('fhij,fihe->fjhe', probs_low, grad_heads, precision=highest)
    grad_probs = jnp.einsum('fihe,fjhe->fhij', grad_heads, to_heads(values, head_count), precision=highest)
    inner = lax.optimization_barrier(jnp.sum(probs * grad_probs, axis=-1, keepdims=True))
    grad_scores = rounded(probs * (grad_probs - inner) * factor).astype(jnp.float32)
    grad_queries = jnp.einsum('fhij,fjhe->fihe', grad_scores, to_heads(key_rows, head_count), precision=highest)
    grad_keys = jnp.einsum('fhij,fihe->fjhe', grad_scores, to_heads(queries, head_count), precision=highest)
    return (rounded(grad_queries.reshape(shape_full)), rounded(grad_keys.reshape(shape_full)), rounded(grad_values.reshape(shape_full)))

def block_pass(pieces, norm_gain, w_qkv, w_out):
    inputs, grad_out = pieces
    columns = inputs.shape[2]
    wide_in = inputs.astype(jnp.float32)
    inverse_rms = lax.rsqrt(lax.optimization_barrier(jnp.mean(wide_in * wide_in, axis=-1, keepdims=True)) + epsilon)
    normed = rounded(wide_in * inverse_rms * norm_gain)
    projected = rounded(per_codebook(normed, w_qkv))
    queries = projected[:, :, :columns]
    key_rows = projected[:, :, columns:2 * columns]
    values = projected[:, :, 2 * columns:]
    probs = attention_probs(queries, key_rows, HEADS)
    probs_low = rounded(probs).astype(jnp.float32)
    mixed = jnp.einsum('fhij,fjhe->fihe', probs_low, to_heads(values, HEADS), precision=highest)
    context = rounded(mixed.reshape(inputs.shape))
    outputs = (wide_in + per_codebook(context, w_out)).astype(jnp.bfloat16)
    grad_context = rounded(per_codebook_back(grad_out, w_out))
    grad_queries, grad_keys, grad_values = attention_grads(queries, key_rows, values, grad_context, HEADS)
    grad_qkv = jnp.concatenate([grad_queries, grad_keys, grad_values], axis=-1)
    scaled = per_codebook_back(grad_qkv, w_qkv) * norm_gain
    inner = lax.optimization_barrier(jnp.mean(scaled * wide_in, axis=-1, keepdims=True))
    grad_in = grad_out.astype(jnp.float32) + inverse_rms * (scaled - wide_in * inverse_rms * inverse_rms * inner)
    return (outputs, grad_in.astype(jnp.bfloat16))

def reference(inputs, norm_gain, w_qkv, w_out, grad_out):
    blocks = FRAMES // FR_DEV
    shape_blocks = (blocks, FR_DEV) + inputs.shape[1:]
    wide_qkv = w_qkv.astype(jnp.float32)
    wide_out = w_out.astype(jnp.float32)
    outputs, grad_in = lax.map(lambda pieces: block_pass(pieces, norm_gain, wide_qkv, wide_out), (inputs.reshape(shape_blocks), grad_out.reshape(shape_blocks)))
    return (outputs.reshape(inputs.shape), grad_in.reshape(inputs.shape))
```

```python
import jax
import jax.numpy as jnp
from jax import lax
from jax.experimental import pallas as pl
from jax.experimental.pallas import tpu as pltpu
from jax.sharding import PartitionSpec as P

D = 1024
CB = 16
FR = 256
FG = FR // CB
HALF = D // 2
EPS = 1e-05
BF = jnp.bfloat16
F32 = jnp.float32
NT = (((1,), (1,)), ((), ()))
NN = (((1,), (0,)), ((), ()))
TN = (((0,), (0,)), ((), ()))


def dot(a, b, dims):
    return lax.dot_general(a, b, dims, preferred_element_type=F32)


def kernel(
    x_ref, gain_ref, wqkv_ref, wout_ref, g_ref, out_ref, gin_ref,
    w, normed, fwd, got, back, home, gn,
    gsend, grecv, lsem, fsend, frecv, bsend, brecv,
):
    cb = lax.axis_index("cb")
    fr = lax.axis_index("frame")
    x, y, zh = fr // 8, (fr // 2) % 4, fr % 2
    xr, xl = (x + 1) % 4, (x + 3) % 4
    yr, yl = (y + 1) % 4, (y + 3) % 4

    def at(xx, yy, zz):
        return {"frame": (xx * 4 + yy) * 2 + zz}

    barrier = pltpu.get_barrier_semaphore()
    for peer in (at(x, y, 1 - zh), at(xr, y, zh), at(xl, y, zh), at(x, yr, zh), at(x, yl, zh)):
        pl.semaphore_signal(barrier, inc=1, device_id=peer)

    @pl.loop(1, CB)
    def _(j):
        pl.semaphore_signal(barrier, inc=1, device_id={"cb": (cb + j) % CB})

    pl.semaphore_wait(barrier, 5 + CB - 1)

    def shard(p):
        if p == 0:
            return wout_ref
        return wqkv_ref.at[:, pl.ds((3 - p) * D, D)]

    def remote(src, dst, p, s, peer):
        return pltpu.make_async_remote_copy(
            src_ref=src, dst_ref=dst, send_sem=gsend.at[p, s], recv_sem=grecv.at[p, s],
            device_id=peer, device_id_type=pl.DeviceIdType.MESH,
        )

    cols = (pl.ds(0, HALF), pl.ds(HALF, HALF))
    copies = {}

    def start(key, copy):
        copy.start()
        copies[key] = copy

    def begin(p):
        own = w.at[p, x, y, pl.ds(zh * 32, 32), :]
        start((p, 0), remote(shard(p), own, p, 0, at(x, y, 1 - zh)))
        local = pltpu.make_async_copy(shard(p), own, lsem.at[p])
        local.start()
        copies[p] = local

    def tick0(p):
        copies[p].wait()
        copies[p, 0].wait_recv()
        for h, right, left in ((0, at(xr, y, zh), at(xl, y, zh)), (1, at(x, yr, zh), at(x, yl, zh))):
            block = w.at[p, x, y, :, cols[h]]
            start((p, 1 + 4 * h), remote(block, block, p, 1 + 4 * h, right))
            start((p, 2 + 4 * h), remote(block, block, p, 2 + 4 * h, left))

    def tick1(p):
        for h, right, left in ((0, at(xr, y, zh), at(xl, y, zh)), (1, at(x, yr, zh), at(x, yl, zh))):
            copies[p, 1 + 4 * h].wait_recv()
            fx, fy = ((xl, y), (x, yl))[h]
            block = w.at[p, fx, fy, pl.ds(0, 32), cols[h]]
            start((p, 3 + 4 * h), remote(block, block, p, 3 + 4 * h, right))
        for h, right, left in ((0, at(xr, y, zh), at(xl, y, zh)), (1, at(x, yr, zh), at(x, yl, zh))):
            copies[p, 2 + 4 * h].wait_recv()
            fx, fy = ((xr, y), (x, yr))[h]
            block = w.at[p, fx, fy, pl.ds(32, 32), cols[h]]
            start((p, 4 + 4 * h), remote(block, block, p, 4 + 4 * h, left))

    def line(p, h, pos, part):
        span = (slice(None), pl.ds(0, 2), pl.ds(2, 2))[part]
        if h == 0:
            return w.at[p, span, pos, :, cols[0]]
        return w.at[p, pos, span, :, cols[1]]

    def tick2(p):
        for h in range(2):
            copies[p, 3 + 4 * h].wait_recv()
            copies[p, 4 + 4 * h].wait_recv()
            right, left = ((at(x, yr, zh), at(x, yl, zh)), (at(xr, y, zh), at(xl, y, zh)))[h]
            block = line(p, h, (y, x)[h], 0)
            start((p, 9 + 4 * h), remote(block, block, p, 9 + 4 * h, right))
            start((p, 10 + 4 * h), remote(block, block, p, 10 + 4 * h, left))

    def tick3(p):
        for h in range(2):
            right, left = ((at(x, yr, zh), at(x, yl, zh)), (at(xr, y, zh), at(xl, y, zh)))[h]
            copies[p, 9 + 4 * h].wait_recv()
            block = line(p, h, (yl, xl)[h], 1)
            start((p, 11 + 4 * h), remote(block, block, p, 11 + 4 * h, right))
            copies[p, 10 + 4 * h].wait_recv()
            block = line(p, h, (yr, xr)[h], 2)
            start((p, 12 + 4 * h), remote(block, block, p, 12 + 4 * h, left))

    def tick4(p):
        for s in (11, 12, 15, 16):
            copies[p, s].wait_recv()

    def exchange(src, dst, ssem, rsem, t, c):
        part = cols[c]

        @pl.loop(0, CB)
        def _(j):
            peer = (cb + 8 + j) % CB

            @pl.when(j != 8)
            def _():
                pltpu.make_async_remote_copy(
                    src_ref=src.at[t, peer, :, part], dst_ref=dst.at[t, cb, :, part],
                    send_sem=ssem.at[t, c], recv_sem=rsem.at[t, c],
                    device_id={"cb": peer}, device_id_type=pl.DeviceIdType.MESH,
                ).start()

        pltpu.make_async_copy(
            src.at[t, cb, :, part], dst.at[t, cb, :, part], rsem.at[t, c]
        ).start()

    def arrived(dst, rsem, t, c):
        whole = dst.at[t, :, :, cols[c]]
        pltpu.make_async_copy(whole, whole, rsem.at[t, c]).wait()

    def sent(src, ssem, t, c):
        most = src.at[t, pl.ds(0, CB - 1), :, cols[c]]
        pltpu.make_async_copy(most, most, ssem.at[t, c]).wait()

    def project(p):
        for c in range(2):

            @pl.loop(0, 2)
            def _(i):
                col = pl.multiple_of((2 * c + i) * 256, 256)
                if p == 0:
                    tile = dot(g_ref[...], w[0, 2 * c + i].reshape(256, D), NT)
                else:
                    tile = dot(normed[...], w[p, :, :, :, pl.ds(col, 256)].reshape(D, 256), NN)
                fwd[p, :, :, pl.ds(col, 256)] = tile.astype(BF).reshape(CB, FG, 256)

            exchange(fwd, got, fsend, frecv, p, c)

    for p in range(4):
        begin(p)

    @pl.loop(0, 8)
    def _(i):
        rows = pl.ds(pl.multiple_of(i * 32, 32), 32)
        wide = x_ref[rows, :].astype(F32)
        r = lax.rsqrt(jnp.mean(wide * wide, axis=-1, keepdims=True) + EPS)
        normed[rows, :] = (wide * r * gain_ref[...]).astype(BF)

    tick0(0), tick1(0), tick2(0), tick0(1)
    tick3(0), tick1(1), tick4(0)
    project(0)
    tick2(1), tick0(2)
    tick3(1), tick1(2), tick4(1)
    project(1)
    tick2(2), tick0(3)
    tick3(2), tick1(3), tick4(2)
    project(2)
    tick2(3), tick3(3), tick4(3)
    project(3)

    ri = lax.broadcasted_iota(jnp.int32, (FR, FR), 0)
    ci = lax.broadcasted_iota(jnp.int32, (FR, FR), 1)
    seen = jnp.logical_and((ri & (FG - 1)) == (ci & (FG - 1)), ri >= ci)
    low = lax.broadcasted_iota(jnp.int32, (FR, 128), 1) < 64
    zero = jnp.zeros((FR, 128), BF)

    for c in range(2):
        for t in range(4):
            arrived(got, frecv, t, c)

        @pl.loop(0, 4)
        def _(i):
            part = pl.ds(pl.multiple_of(c * HALF + i * 128, 128), 128)
            gc, v, k, q = (got[t, :, :, part].reshape(FR, 128) for t in range(4))
            results = []
            for mine in (low, jnp.logical_not(low)):
                scores = jnp.where(seen, dot(jnp.where(mine, q, zero), k, NT) * 0.125, -jnp.inf)
                e = jnp.exp(scores - jnp.max(scores, axis=-1, keepdims=True))
                probs = e / jnp.sum(e, axis=-1, keepdims=True)
                rough = probs.astype(BF)
                gp = dot(jnp.where(mine, gc, zero), v, NT)
                inner = jnp.sum(probs * gp, axis=-1, keepdims=True)
                gs = (probs * (gp - inner) * 0.125).astype(BF)
                results.append((dot(gs, k, NN), dot(gs, q, TN), dot(rough, gc, TN), dot(rough, v, NN)))
            for t in range(4):
                both = jnp.where(low, results[0][t], results[1][t])
                back[t, :, :, part] = both.astype(BF).reshape(CB, FG, 128)

        for t in range(4):
            exchange(back, home, bsend, brecv, t, c)

    for t in range(3):
        for c in range(2):
            arrived(home, brecv, t, c)

        @pl.loop(0, 4)
        def _(i):
            part = pl.ds(pl.multiple_of(i * 256, 256), 256)
            tile = dot(home[t].reshape(FR, D), w[3 - t, i].reshape(256, D), NT)
            gn[:, part] = tile if t == 0 else gn[:, part] + tile

    @pl.loop(0, 8)
    def _(i):
        rows = pl.ds(pl.multiple_of(i * 32, 32), 32)
        wide = x_ref[rows, :].astype(F32)
        r = lax.rsqrt(jnp.mean(wide * wide, axis=-1, keepdims=True) + EPS)
        s = gn[rows, :] * gain_ref[...]
        inner = jnp.mean(s * wide, axis=-1, keepdims=True)
        gin_ref[rows, :] = (g_ref[rows, :].astype(F32) + r * (s - wide * (r * r * inner))).astype(BF)

    for c in range(2):
        arrived(home, brecv, 3, c)

    @pl.loop(0, 4)
    def _(i):
        part = pl.ds(pl.multiple_of(i * 256, 256), 256)
        tile = dot(home[3].reshape(FR, D), w[0, :, :, :, part].reshape(D, 256), NN)
        out_ref[:, part] = (x_ref[:, part].astype(F32) + tile).astype(BF)

    for p in range(4):
        for s in range(17):
            copies[p, s].wait_send()
        for c in range(2):
            sent(fwd, fsend, p, c)
            sent(back, bsend, p, c)


def body(inputs, norm_gain, w_qkv, w_out, grad_out):
    vmem = pl.BlockSpec(memory_space=pltpu.VMEM)
    block = (4, CB, FG, D)
    outputs, grad_in = pl.pallas_call(
        kernel,
        out_shape=[jax.ShapeDtypeStruct((FR, D), BF)] * 2,
        in_specs=[vmem] * 5,
        out_specs=[vmem] * 2,
        scratch_shapes=[
            pltpu.VMEM((4, 4, 4, 64, D), BF),
            pltpu.VMEM((FR, D), BF),
            pltpu.VMEM(block, BF),
            pltpu.VMEM(block, BF),
            pltpu.VMEM(block, BF),
            pltpu.VMEM(block, BF),
            pltpu.VMEM((FR, D), F32),
            pltpu.SemaphoreType.DMA((4, 17)),
            pltpu.SemaphoreType.DMA((4, 17)),
            pltpu.SemaphoreType.DMA((4,)),
            pltpu.SemaphoreType.DMA((4, 2)),
            pltpu.SemaphoreType.DMA((4, 2)),
            pltpu.SemaphoreType.DMA((4, 2)),
            pltpu.SemaphoreType.DMA((4, 2)),
        ],
        compiler_params=pltpu.CompilerParams(
            collective_id=0, has_side_effects=True, vmem_limit_bytes=60 * 2**20
        ),
    )(
        inputs.reshape(FR, D),
        norm_gain.reshape(1, D),
        w_qkv.reshape(32, 3 * D),
        w_out.reshape(32, D),
        grad_out.reshape(FR, D),
    )
    return outputs.reshape(FR, 1, D), grad_in.reshape(FR, 1, D)


def solution(mesh):
    return jax.shard_map(
        body,
        mesh=mesh,
        in_specs=(
            P("frame", "cb", None),
            P(),
            P("cb", "frame", None),
            P("cb", "frame", None),
            P("frame", "cb", None),
        ),
        out_specs=(P("frame", "cb", None), P("frame", "cb", None)),
        check_vma=False,
    )
```

```python
import functools

import jax
import jax.numpy as jnp
from jax import lax
from jax.experimental import pallas as pl
from jax.experimental.pallas import tpu as pltpu
from jax.sharding import PartitionSpec as P

D = 1024
CB = 16
FR = 256
GR = 8
FG = FR // GR
CH = 256
NCH = D // CH
EPS = 1e-05
BF = jnp.bfloat16
F32 = jnp.float32
NT = (((1,), (1,)), ((), ()))
NN = (((1,), (0,)), ((), ()))
TN = (((0,), (0,)), ((), ()))


def dot(a, b, dims):
    return lax.dot_general(a, b, dims, preferred_element_type=F32)


def kernel(
    x_hbm, gain_ref, wqkv_ref, wout_ref, g_hbm, out_ref, gin_ref,
    x_ref, g_ref, w, normed, fwd, got, gotx, back, backx, home, homex, gn, total,
    zsend, zrecv, gsend, grecv, lsem, isem, fsend, frecv, fxsend, fxrecv, bsend, brecv, bxsend, bxrecv,
):
    cb = lax.axis_index("cb")
    fr = lax.axis_index("frame")
    upper, me = cb // GR, cb % GR
    x, y, zh = fr // 8, (fr // 2) % 4, fr % 2
    xr, xl = (x + 1) % 4, (x + 3) % 4
    yr, yl = (y + 1) % 4, (y + 3) % 4

    def at(xx, yy, zz):
        return {"frame": (xx * 4 + yy) * 2 + zz}

    loads = [
        pltpu.make_async_copy(x_hbm, x_ref, isem.at[0]),
        pltpu.make_async_copy(g_hbm, g_ref, isem.at[1]),
    ]
    for load in loads:
        load.start()

    barrier = pltpu.get_barrier_semaphore()
    for peer in (at(x, y, 1 - zh), at(xr, y, zh), at(xl, y, zh), at(x, yr, zh), at(x, yl, zh)):
        pl.semaphore_signal(barrier, inc=1, device_id=peer)

    @pl.loop(1, CB)
    def _(j):
        pl.semaphore_signal(barrier, inc=1, device_id={"cb": (cb + j) % CB})

    ways_x, ways_y = (at(xr, y, zh), at(xl, y, zh)), (at(x, yr, zh), at(x, yl, zh))
    copies = {}

    def keep(m):
        shard = wqkv_ref.at[:, pl.ds((3 - m) * D, D)] if m else wout_ref
        local = pltpu.make_async_copy(shard, w.at[m, x, y, pl.ds(zh * 32, 32), :], lsem.at[m])
        local.start()
        copies[m] = local

    def swap(m, j):
        key = 0 if m == 0 else 1 + 3 * j + m - 1
        width = CH if m else D
        copy = pltpu.make_async_remote_copy(
            src_ref=wqkv_ref.at[:, pl.ds((3 - m) * D + j * CH, CH)] if m else wout_ref,
            dst_ref=w.at[m, x, y, pl.ds(zh * 32, 32), pl.ds(j * CH, width)],
            send_sem=zsend.at[key], recv_sem=zrecv.at[key],
            device_id=at(x, y, 1 - zh), device_id_type=pl.DeviceIdType.MESH,
        )
        copy.start()
        copies["z", m, j] = copy

    def remote(key, src, dst, peer):
        copy = pltpu.make_async_remote_copy(
            src_ref=src, dst_ref=dst, send_sem=gsend.at[key], recv_sem=grecv.at[key],
            device_id=peer, device_id_type=pl.DeviceIdType.MESH,
        )
        copy.start()
        copies[key] = copy

    def view(p, h, xs, ys, half=None):
        if p in (0, 5):
            start = 32 * (zh if p == 0 else 1 - zh)
            rows = pl.ds(start, 32) if half is None else pl.ds(start + 16 * half, 16)
            return w.at[0, xs, ys, rows, pl.ds(h * 512, 512)]
        rows = slice(None) if half is None else pl.ds(32 * half, 32)
        return w.at[pl.ds(1, 3), xs, ys, rows, pl.ds((p - 1) * CH + h * 128, 128)]

    def landed(j):
        for m in (1, 2, 3):
            if j == 0:
                copies[m].wait()
            copies["z", m, j].wait_recv()

    def tick0(p):
        for h, ways in ((0, ways_x), (1, ways_y)):
            block = view(p, h, x, y)
            remote((p, 1 + 4 * h), block, block, ways[0])
            remote((p, 2 + 4 * h), block, block, ways[1])

    def tick1(p):
        for h, ways in ((0, ways_x), (1, ways_y)):
            copies[p, 1 + 4 * h].wait_recv()
            block = view(p, h, *((xl, y), (x, yl))[h], 0)
            remote((p, 3 + 4 * h), block, block, ways[0])
        for h, ways in ((0, ways_x), (1, ways_y)):
            copies[p, 2 + 4 * h].wait_recv()
            block = view(p, h, *((xr, y), (x, yr))[h], 1)
            remote((p, 4 + 4 * h), block, block, ways[1])

    def line(p, h, pos, span):
        return view(p, h, *((span, pos), (pos, span))[h])

    def tick2(p):
        for h, ways in ((0, ways_y), (1, ways_x)):
            copies[p, 3 + 4 * h].wait_recv()
            copies[p, 4 + 4 * h].wait_recv()
            block = line(p, h, (y, x)[h], slice(None))
            remote((p, 9 + 4 * h), block, block, ways[0])
            remote((p, 10 + 4 * h), block, block, ways[1])

    def tick3(p):
        for h, ways in ((0, ways_y), (1, ways_x)):
            copies[p, 9 + 4 * h].wait_recv()
            block = line(p, h, (yl, xl)[h], pl.ds(0, 2))
            remote((p, 11 + 4 * h), block, block, ways[0])
        for h, ways in ((0, ways_y), (1, ways_x)):
            copies[p, 10 + 4 * h].wait_recv()
            block = line(p, h, (yr, xr)[h], pl.ds(2, 2))
            remote((p, 12 + 4 * h), block, block, ways[1])

    def tick4(p):
        for s in (11, 12, 15, 16):
            copies[p, s].wait_recv()

    def chunk(j):
        return pl.ds(j * CH, CH)

    def exchange(src, dst, ssem, rsem, t, j, way=None):
        @pl.loop(0, GR)
        def _(i):
            peer = (me + 4 + i) % GR
            wanted = {None: peer != me, 0: peer < me, 1: peer > me}[way]

            @pl.when(wanted)
            def _():
                pltpu.make_async_remote_copy(
                    src_ref=src.at[t, j, peer], dst_ref=dst.at[t, j, me],
                    send_sem=ssem.at[t, j], recv_sem=rsem.at[t, j],
                    device_id={"cb": upper * GR + peer}, device_id_type=pl.DeviceIdType.MESH,
                ).start()

        if way != 1:
            pltpu.make_async_copy(src.at[t, j, me], dst.at[t, j, me], rsem.at[t, j]).start()

    def across(src, dst, ssem, rsem, t, t2, j):
        @pl.loop(0, GR)
        def _(i):
            peer = (me + 4 + i) % GR
            pltpu.make_async_remote_copy(
                src_ref=src.at[t, j, peer], dst_ref=dst.at[t2, j, me],
                send_sem=ssem.at[t2, j], recv_sem=rsem.at[t2, j],
                device_id={"cb": (1 - upper) * GR + peer}, device_id_type=pl.DeviceIdType.MESH,
            ).start()

    def drain(buf, sem, t, j, count=GR):
        whole = buf.at[t, j, pl.ds(0, count)]
        pltpu.make_async_copy(whole, whole, sem.at[t, j]).wait()

    def project(m, j):
        if m == 0:
            tile = dot(g_ref[...], w[0, j].reshape(CH, D), NT)
        else:
            tile = dot(normed[...], w[m, :, :, :, chunk(j)].reshape(D, CH), NN)
        fwd[m, j] = tile.astype(BF).reshape(GR, FG, CH)

        if m in (1, 2):
            @pl.when(upper == 0)
            def _():
                across(fwd, gotx, fxsend, fxrecv, m, m - 1, j)

        exchange(fwd, got, fsend, frecv, m, j)

    def projections(j):
        for m in (1, 2, 3):
            project(m, j)

    ri = lax.broadcasted_iota(jnp.int32, (FR, FR), 0)
    ci = lax.broadcasted_iota(jnp.int32, (FR, FR), 1)
    low = lax.broadcasted_iota(jnp.int32, (FR, 128), 1) < 64
    zero = jnp.zeros((FR, 128), BF)

    def heads(j, wide):
        @pl.loop(0, 2)
        def _(i):
            part = pl.ds(pl.multiple_of(i * 128, 128), 128)
            frame = (ri & (FG - 1)) == (ci & (FG - 1))
            masks = [jnp.logical_and(frame, ri >= ci)]
            gc, v, k, q = (got[t, j, :, :, part].reshape(FR, 128) for t in range(4))
            vs, ks = [v], [k]
            if wide:
                masks.append(frame)
                vs.append(gotx[0, j, :, :, part].reshape(FR, 128))
                ks.append(gotx[1, j, :, :, part].reshape(FR, 128))
            results = []
            for mine in (low, jnp.logical_not(low)):
                q1, gc1 = jnp.where(mine, q, zero), jnp.where(mine, gc, zero)
                scores = [
                    jnp.where(seen, dot(q1, kk, NT) * 0.125, -jnp.inf) for seen, kk in zip(masks, ks)
                ]
                top = functools.reduce(jnp.maximum, [jnp.max(s, axis=-1, keepdims=True) for s in scores])
                e = [jnp.exp(s - top) for s in scores]
                norm = sum(jnp.sum(s, axis=-1, keepdims=True) for s in e)
                probs = [s / norm for s in e]
                rough = [s.astype(BF) for s in probs]
                gp = [dot(gc1, vv, NT) for vv in vs]
                inner = sum(jnp.sum(a * b, axis=-1, keepdims=True) for a, b in zip(probs, gp))
                gs = [(a * (b - inner) * 0.125).astype(BF) for a, b in zip(probs, gp)]
                found = [
                    sum(dot(a, b, NN) for a, b in zip(gs, ks)),
                    dot(gs[0], q, TN),
                    dot(rough[0], gc, TN),
                    sum(dot(a, b, NN) for a, b in zip(rough, vs)),
                ]
                if wide:
                    found += [dot(gs[1], q, TN), dot(rough[1], gc, TN)]
                results.append(found)
            for t, (a, b) in enumerate(zip(*results)):
                both = jnp.where(low, a, b).astype(BF).reshape(GR, FG, 128)
                if t < 4:
                    back[t, j, :, :, part] = both
                else:
                    backx[t - 4, j, :, :, part] = both

    def attend(j):
        for t in range(4):
            drain(got, frecv, t, j)

        @pl.when(upper == 0)
        def _():
            heads(j, False)

        @pl.when(upper == 1)
        def _():
            for t in range(2):
                drain(gotx, fxrecv, t, j)
            heads(j, True)
            for t in range(2):
                across(backx, homex, bxsend, bxrecv, t, t, j)

        for t in range(4):
            exchange(back, home, bsend, brecv, t, j, 0)

    def finish(j):
        for t in range(3):
            drain(home, brecv, t, j)

        @pl.when(upper == 0)
        def _():
            for t in range(2):
                drain(homex, bxrecv, t, j)
                home[t + 1, j] = (home[t + 1, j].astype(F32) + homex[t, j].astype(F32)).astype(BF)

        @pl.loop(0, 4)
        def _(i):
            part = pl.ds(pl.multiple_of(i * 256, 256), 256)
            tile = sum(
                dot(home[t, j].reshape(FR, CH), w[3 - t, i, :, :, chunk(j)].reshape(256, CH), NT)
                for t in range(3)
            )
            gn[:, part] = tile if j == 0 else gn[:, part] + tile

        if j == NCH - 1:
            @pl.loop(0, 8)
            def _(i):
                rows = pl.ds(pl.multiple_of(i * 32, 32), 32)
                wide = x_ref[rows, :].astype(F32)
                r = lax.rsqrt(jnp.mean(wide * wide, axis=-1, keepdims=True) + EPS)
                s = gn[rows, :] * gain_ref[...]
                inner = jnp.mean(s * wide, axis=-1, keepdims=True)
                gin_ref[rows, :] = (
                    g_ref[rows, :].astype(F32) + r * (s - wide * (r * r * inner))
                ).astype(BF)

        drain(home, brecv, 3, j)

        @pl.loop(0, 4)
        def _(i):
            part = pl.ds(pl.multiple_of(i * 256, 256), 256)
            tile = dot(
                home[3, j].reshape(FR, CH), w[0, j, :, :, part].reshape(CH, 256), NN
            )
            tile = tile + (x_ref[:, part].astype(F32) if j == 0 else total[:, part])
            if j == NCH - 1:
                out_ref[:, part] = tile.astype(BF)
            else:
                total[:, part] = tile

    for m in range(4):
        keep(m)

    loads[0].wait()

    @pl.loop(0, 8)
    def _(i):
        rows = pl.ds(pl.multiple_of(i * 32, 32), 32)
        wide = x_ref[rows, :].astype(F32)
        r = lax.rsqrt(jnp.mean(wide * wide, axis=-1, keepdims=True) + EPS)
        normed[rows, :] = (wide * r * gain_ref[...]).astype(BF)

    loads[1].wait()
    copies[0].wait()
    pl.semaphore_wait(barrier, 5 + CB - 1)

    swap(0, 0)
    tick0(0)
    for m in (1, 2, 3):
        swap(m, 0)
    tick1(0)
    copies["z", 0, 0].wait_recv()
    tick0(5), tick2(0), tick1(5), tick3(0), tick2(5)
    for j in range(1, NCH):
        for m in (1, 2, 3):
            swap(m, j)
    landed(0)
    tick0(1), tick4(0), tick3(5), tick1(1), tick4(5)
    for j in range(NCH):
        project(0, j)
    tick2(1), landed(1), tick0(2), tick3(1), tick1(2), tick4(1)
    projections(0)
    tick2(2), landed(2), tick0(3), tick3(2), tick1(3), tick4(2)
    projections(1)
    tick2(3), landed(3), tick0(4), tick3(3), tick1(4), tick4(3)
    projections(2)
    tick2(4), tick3(4), tick4(4)
    projections(3)
    attend(0)
    attend(1)
    attend(2)
    attend(3)
    for j in range(NCH):
        for t in range(4):
            exchange(back, home, bsend, brecv, t, j, 1)
    finish(0)
    finish(1)
    finish(2)
    finish(3)

    copies["z", 0, 0].wait_send()
    for m in range(4):
        for j in range(NCH):
            if m:
                copies["z", m, j].wait_send()
            drain(fwd, fsend, m, j, GR - 1)
            drain(back, bsend, m, j, GR - 1)
    for p in range(2 + NCH):
        for s in range(1, 17):
            copies[p, s].wait_send()

    @pl.when(upper == 0)
    def _():
        for t in range(2):
            for j in range(NCH):
                drain(gotx, fxsend, t, j)

    @pl.when(upper == 1)
    def _():
        for t in range(2):
            for j in range(NCH):
                drain(homex, bxsend, t, j)


def body(inputs, norm_gain, w_qkv, w_out, grad_out):
    vmem, hbm = pl.BlockSpec(memory_space=pltpu.VMEM), pl.BlockSpec(memory_space=pl.ANY)
    four, two = pltpu.VMEM((4, NCH, GR, FG, CH), BF), pltpu.VMEM((2, NCH, GR, FG, CH), BF)
    sem4, sem2 = pltpu.SemaphoreType.DMA((4, NCH)), pltpu.SemaphoreType.DMA((2, NCH))
    outputs, grad_in = pl.pallas_call(
        kernel,
        out_shape=[jax.ShapeDtypeStruct((FR, D), BF)] * 2,
        in_specs=[hbm, vmem, hbm, hbm, hbm],
        out_specs=[vmem] * 2,
        scratch_shapes=[
            pltpu.VMEM((FR, D), BF),
            pltpu.VMEM((FR, D), BF),
            pltpu.VMEM((4, 4, 4, 64, D), BF),
            pltpu.VMEM((FR, D), BF),
            four, four, two, four, two, four, two,
            pltpu.VMEM((FR, D), F32),
            pltpu.VMEM((FR, D), F32),
            pltpu.SemaphoreType.DMA((1 + 3 * NCH,)),
            pltpu.SemaphoreType.DMA((1 + 3 * NCH,)),
            pltpu.SemaphoreType.DMA((2 + NCH, 17)),
            pltpu.SemaphoreType.DMA((2 + NCH, 17)),
            pltpu.SemaphoreType.DMA((4,)),
            pltpu.SemaphoreType.DMA((2,)),
            sem4, sem4, sem2, sem2, sem4, sem4, sem2, sem2,
        ],
        compiler_params=pltpu.CompilerParams(
            collective_id=0, has_side_effects=True, vmem_limit_bytes=60 * 2**20
        ),
    )(
        inputs.reshape(FR, D),
        norm_gain.reshape(1, D),
        w_qkv.reshape(32, 3 * D),
        w_out.reshape(32, D),
        grad_out.reshape(FR, D),
    )
    return outputs.reshape(FR, 1, D), grad_in.reshape(FR, 1, D)


def solution(mesh):
    return jax.shard_map(
        body,
        mesh=mesh,
        in_specs=(
            P("frame", "cb", None),
            P(),
            P("cb", "frame", None),
            P("cb", "frame", None),
            P("frame", "cb", None),
        ),
        out_specs=(P("frame", "cb", None), P("frame", "cb", None)),
        check_vma=False,
    )
```

```python
import functools

import jax
import jax.numpy as jnp
from jax import lax
from jax.experimental import pallas as pl
from jax.experimental.pallas import tpu as pltpu
from jax.sharding import PartitionSpec as P

D = 1024
CB = 16
FR = 256
GR = 8
FG = FR // GR
CH = 256
NCH = D // CH
LOW = 1
EPS = 1e-05
BF = jnp.bfloat16
F32 = jnp.float32
NT = (((1,), (1,)), ((), ()))
NN = (((1,), (0,)), ((), ()))
TN = (((0,), (0,)), ((), ()))


def dot(a, b, dims):
    return lax.dot_general(a, b, dims, preferred_element_type=F32)


def kernel(
    x_hbm, gain_ref, wqkv_ref, wout_ref, g_hbm, out_ref, gin_ref,
    x_ref, g_ref, w, normed, fwd, got, gotx, gotl, back, backx, backl, home, homex, gn, total,
    zsend, zrecv, gsend, grecv, lsem, isem, fsend, frecv, fxsend, fxrecv, flsend, flrecv,
    bsend, brecv, bxsend, bxrecv, blsend,
):
    cb = lax.axis_index("cb")
    fr = lax.axis_index("frame")
    upper, me = cb // GR, cb % GR
    x, y, zh = fr // 8, (fr // 2) % 4, fr % 2
    xr, xl = (x + 1) % 4, (x + 3) % 4
    yr, yl = (y + 1) % 4, (y + 3) % 4

    def at(xx, yy, zz):
        return {"frame": (xx * 4 + yy) * 2 + zz}

    loads = [
        pltpu.make_async_copy(x_hbm, x_ref, isem.at[0]),
        pltpu.make_async_copy(g_hbm, g_ref, isem.at[1]),
    ]
    for load in loads:
        load.start()

    barrier = pltpu.get_barrier_semaphore()
    for peer in (at(x, y, 1 - zh), at(xr, y, zh), at(xl, y, zh), at(x, yr, zh), at(x, yl, zh)):
        pl.semaphore_signal(barrier, inc=1, device_id=peer)

    @pl.loop(1, CB)
    def _(j):
        pl.semaphore_signal(barrier, inc=1, device_id={"cb": (cb + j) % CB})

    ways_x, ways_y = (at(xr, y, zh), at(xl, y, zh)), (at(x, yr, zh), at(x, yl, zh))
    copies = {}

    def keep(m):
        shard = wqkv_ref.at[:, pl.ds((3 - m) * D, D)] if m else wout_ref
        local = pltpu.make_async_copy(shard, w.at[m, x, y, pl.ds(zh * 32, 32), :], lsem.at[m])
        local.start()
        copies[m] = local

    def swap(m, j):
        key = 0 if m == 0 else 1 + 3 * j + m - 1
        width = CH if m else D
        copy = pltpu.make_async_remote_copy(
            src_ref=wqkv_ref.at[:, pl.ds((3 - m) * D + j * CH, CH)] if m else wout_ref,
            dst_ref=w.at[m, x, y, pl.ds(zh * 32, 32), pl.ds(j * CH, width)],
            send_sem=zsend.at[key], recv_sem=zrecv.at[key],
            device_id=at(x, y, 1 - zh), device_id_type=pl.DeviceIdType.MESH,
        )
        copy.start()
        copies["z", m, j] = copy

    def remote(key, src, dst, peer):
        copy = pltpu.make_async_remote_copy(
            src_ref=src, dst_ref=dst, send_sem=gsend.at[key], recv_sem=grecv.at[key],
            device_id=peer, device_id_type=pl.DeviceIdType.MESH,
        )
        copy.start()
        copies[key] = copy

    def view(p, h, xs, ys, half=None):
        if p in (0, 5):
            start = 32 * (zh if p == 0 else 1 - zh)
            rows = pl.ds(start, 32) if half is None else pl.ds(start + 16 * half, 16)
            return w.at[pl.ds(1, 3), xs, ys, rows, pl.ds(h * 128, 128)]
        rows = slice(None) if half is None else pl.ds(32 * half, 32)
        if p == 1:
            return w.at[0, xs, ys, rows, pl.ds(h * 512, 512)]
        return w.at[pl.ds(1, 3), xs, ys, rows, pl.ds((p - 1) * CH + h * 128, 128)]

    def landed(j):
        for m in (1, 2, 3):
            copies["z", m, j].wait_recv()

    def tick0(p):
        for h, ways in ((0, ways_x), (1, ways_y)):
            block = view(p, h, x, y)
            remote((p, 1 + 4 * h), block, block, ways[0])
            remote((p, 2 + 4 * h), block, block, ways[1])

    def tick1(p):
        for h, ways in ((0, ways_x), (1, ways_y)):
            copies[p, 1 + 4 * h].wait_recv()
            block = view(p, h, *((xl, y), (x, yl))[h], 0)
            remote((p, 3 + 4 * h), block, block, ways[0])
        for h, ways in ((0, ways_x), (1, ways_y)):
            copies[p, 2 + 4 * h].wait_recv()
            block = view(p, h, *((xr, y), (x, yr))[h], 1)
            remote((p, 4 + 4 * h), block, block, ways[1])

    def line(p, h, pos, span):
        return view(p, h, *((span, pos), (pos, span))[h])

    def tick2(p):
        for h, ways in ((0, ways_y), (1, ways_x)):
            copies[p, 3 + 4 * h].wait_recv()
            copies[p, 4 + 4 * h].wait_recv()
            block = line(p, h, (y, x)[h], slice(None))
            remote((p, 9 + 4 * h), block, block, ways[0])
            remote((p, 10 + 4 * h), block, block, ways[1])

    def tick3(p):
        for h, ways in ((0, ways_y), (1, ways_x)):
            copies[p, 9 + 4 * h].wait_recv()
            block = line(p, h, (yl, xl)[h], pl.ds(0, 2))
            remote((p, 11 + 4 * h), block, block, ways[0])
        for h, ways in ((0, ways_y), (1, ways_x)):
            copies[p, 10 + 4 * h].wait_recv()
            block = line(p, h, (yr, xr)[h], pl.ds(2, 2))
            remote((p, 12 + 4 * h), block, block, ways[1])

    def tick4(p):
        for s in (11, 12, 15, 16):
            copies[p, s].wait_recv()

    def chunk(j):
        return pl.ds(j * CH, CH)

    def exchange(src, dst, ssem, rsem, t, j, way=None):
        @pl.loop(0, GR)
        def _(i):
            peer = (me + 4 + i) % GR
            wanted = {None: peer != me, 0: peer < me, 1: peer > me}[way]

            @pl.when(wanted)
            def _():
                pltpu.make_async_remote_copy(
                    src_ref=src.at[t, j, peer], dst_ref=dst.at[t, j, me],
                    send_sem=ssem.at[t, j], recv_sem=rsem.at[t, j],
                    device_id={"cb": upper * GR + peer}, device_id_type=pl.DeviceIdType.MESH,
                ).start()

        if way != 1:
            pltpu.make_async_copy(src.at[t, j, me], dst.at[t, j, me], rsem.at[t, j]).start()

    def across(src, dst, ssem, rsem):
        @pl.loop(0, GR)
        def _(i):
            peer = (me + 4 + i) % GR
            pltpu.make_async_remote_copy(
                src_ref=src.at[peer], dst_ref=dst.at[me], send_sem=ssem, recv_sem=rsem,
                device_id={"cb": (1 - upper) * GR + peer}, device_id_type=pl.DeviceIdType.MESH,
            ).start()

    def wait(whole, sem):
        pltpu.make_async_copy(whole, whole, sem).wait()

    def drain(buf, sem, t, j, count=GR):
        wait(buf.at[t, j, pl.ds(0, count)], sem.at[t, j])

    def project(m, j):
        if m == 0:
            tile = dot(g_ref[...], w[0, j].reshape(CH, D), NT)
        else:
            tile = dot(normed[...], w[m, :, :, :, chunk(j)].reshape(D, CH), NN)
        fwd[m, j] = tile.astype(BF).reshape(GR, FG, CH)

        if m in (1, 2):
            @pl.when(upper == int(j == LOW))
            def _():
                across(fwd.at[m, j], gotx.at[m - 1, j], fxsend.at[m - 1, j], fxrecv.at[m - 1, j])
        elif j == LOW:
            @pl.when(upper == 1)
            def _():
                across(fwd.at[m, j], gotl.at[m // 3], flsend.at[m // 3], flrecv.at[m // 3])

        @pl.when(jnp.logical_or(upper == 0, j != LOW))
        def _():
            exchange(fwd, got, fsend, frecv, m, j)

    def projections(j):
        for m in (1, 2, 3):
            project(m, j)

    ri = lax.broadcasted_iota(jnp.int32, (FR, FR), 0)
    ci = lax.broadcasted_iota(jnp.int32, (FR, FR), 1)
    low = lax.broadcasted_iota(jnp.int32, (FR, 128), 1) < 64
    zero = jnp.zeros((FR, 128), BF)

    def grads(mine, masks, q, gc, ks, vs):
        q1, gc1 = jnp.where(mine, q, zero), jnp.where(mine, gc, zero)
        scores = [jnp.where(seen, dot(q1, k, NT) * 0.125, -jnp.inf) for seen, k in zip(masks, ks)]
        top = functools.reduce(jnp.maximum, [jnp.max(s, axis=-1, keepdims=True) for s in scores])
        e = [jnp.exp(s - top) for s in scores]
        norm = sum(jnp.sum(s, axis=-1, keepdims=True) for s in e)
        probs = [s / norm for s in e]
        rough = [s.astype(BF) for s in probs]
        gp = [dot(gc1, v, NT) for v in vs]
        inner = sum(jnp.sum(a * b, axis=-1, keepdims=True) for a, b in zip(probs, gp))
        gs = [(a * (b - inner) * 0.125).astype(BF) for a, b in zip(probs, gp)]
        found = [
            sum(dot(a, b, NN) for a, b in zip(gs, ks)),
            dot(gs[0], q, TN),
            dot(rough[0], gc, TN),
            sum(dot(a, b, NN) for a, b in zip(rough, vs)),
        ]
        for a, b in zip(gs[1:], rough[1:]):
            found += [dot(a, q, TN), dot(b, gc, TN)]
        return found

    def heads(j):
        @pl.loop(0, 2)
        def _(i):
            part = pl.ds(pl.multiple_of(i * 128, 128), 128)
            frame = (ri & (FG - 1)) == (ci & (FG - 1))
            causal = jnp.logical_and(frame, ri >= ci)

            def load(*refs):
                return [ref[:, :, part].reshape(FR, 128) for ref in refs]

            def store(refs, results):
                for ref, a, b in zip(refs, *results):
                    ref[:, :, part] = jnp.where(low, a, b).astype(BF).reshape(GR, FG, 128)

            sides = (low, jnp.logical_not(low))
            backs = [back.at[t, j] for t in range(4)]

            def apart(extra):
                gc, v, k, q = load(*(got.at[t, j] for t in range(4)))
                vs, ks, masks = [v], [k], [causal]
                if extra:
                    vx, kx = load(gotx.at[0, j], gotx.at[1, j])
                    vs, ks, masks = [v, vx], [k, kx], [causal, frame]
                store(
                    backs + [backx.at[0, j], backx.at[1, j]] * extra,
                    [grads(mine, masks, q, gc, ks, vs) for mine in sides],
                )

            def together():
                gc, v, k, q = load(*(got.at[t, j] for t in range(4)))
                vh, kh, gch, qh = load(gotx.at[0, j], gotx.at[1, j], gotl.at[0], gotl.at[1])
                results = []
                for mine in sides:
                    a = grads(mine, [causal], q, gc, [k], [v])
                    b = grads(mine, [causal, frame], qh, gch, [kh, k], [vh, v])
                    results.append([a[0], a[1] + b[4], a[2] + b[5], a[3]] + b[:4])
                store(backs + [backl.at[t] for t in range(4)], results)

            if j == LOW:
                together()
            else:
                @pl.when(upper == 0)
                def _():
                    apart(0)

                @pl.when(upper == 1)
                def _():
                    apart(1)

    def attend(j):
        @pl.when(jnp.logical_or(upper == 0, j != LOW))
        def _():
            for t in range(4):
                drain(got, frecv, t, j)

            @pl.when(upper == int(j != LOW))
            def _():
                for t in range(2):
                    drain(gotx, fxrecv, t, j)
                    if j == LOW:
                        wait(gotl.at[t], flrecv.at[t])

            heads(j)
            if j != LOW:
                @pl.when(upper == 1)
                def _():
                    for t in range(2):
                        across(backx.at[t, j], homex.at[t, j], bxsend.at[t, j], bxrecv.at[t, j])

            for t in range(4):
                exchange(back, home, bsend, brecv, t, j, 0)

    def rest(j):
        @pl.when(jnp.logical_or(upper == 0, j != LOW))
        def _():
            for t in range(4):
                exchange(back, home, bsend, brecv, t, j, 1)

    def lift(ts):
        @pl.when(upper == 0)
        def _():
            for t in ts:
                across(backl.at[t], home.at[t, LOW], blsend.at[t], brecv.at[t, LOW])

    def finish(j, first=False, last=False):
        for t in range(3):
            drain(home, brecv, t, j)

        @pl.when(jnp.logical_and(upper == 0, j != LOW))
        def _():
            for t in range(2):
                drain(homex, bxrecv, t, j)
                home[t + 1, j] = (home[t + 1, j].astype(F32) + homex[t, j].astype(F32)).astype(BF)

        @pl.loop(0, 4)
        def _(i):
            part = pl.ds(pl.multiple_of(i * 256, 256), 256)
            tile = sum(
                dot(home[t, j].reshape(FR, CH), w[3 - t, i, :, :, chunk(j)].reshape(256, CH), NT)
                for t in range(3)
            )
            gn[:, part] = tile if first else gn[:, part] + tile

        if last:
            @pl.loop(0, 8)
            def _(i):
                rows = pl.ds(pl.multiple_of(i * 32, 32), 32)
                wide = x_ref[rows, :].astype(F32)
                r = lax.rsqrt(jnp.mean(wide * wide, axis=-1, keepdims=True) + EPS)
                s = gn[rows, :] * gain_ref[...]
                inner = jnp.mean(s * wide, axis=-1, keepdims=True)
                gin_ref[rows, :] = (
                    g_ref[rows, :].astype(F32) + r * (s - wide * (r * r * inner))
                ).astype(BF)

        drain(home, brecv, 3, j)

        @pl.loop(0, 4)
        def _(i):
            part = pl.ds(pl.multiple_of(i * 256, 256), 256)
            tile = dot(
                home[3, j].reshape(FR, CH), w[0, j, :, :, part].reshape(CH, 256), NN
            )
            tile = tile + (x_ref[:, part].astype(F32) if first else total[:, part])
            if last:
                out_ref[:, part] = tile.astype(BF)
            else:
                total[:, part] = tile

    for m in (1, 2, 3, 0):
        keep(m)

    loads[0].wait()

    @pl.loop(0, 8)
    def _(i):
        rows = pl.ds(pl.multiple_of(i * 32, 32), 32)
        wide = x_ref[rows, :].astype(F32)
        r = lax.rsqrt(jnp.mean(wide * wide, axis=-1, keepdims=True) + EPS)
        normed[rows, :] = (wide * r * gain_ref[...]).astype(BF)

    for m in (1, 2, 3):
        copies[m].wait()
    pl.semaphore_wait(barrier, 5 + CB - 1)

    for m in (1, 2, 3):
        swap(m, 0)
    tick0(0)
    swap(0, 0)
    tick1(0)
    landed(0)
    tick0(5), tick2(0), tick1(5), tick3(0), tick2(5)
    for j in range(1, NCH):
        for m in (1, 2, 3):
            swap(m, j)
    loads[1].wait()
    copies[0].wait()
    copies["z", 0, 0].wait_recv()
    tick0(1), tick4(0), tick3(5), tick1(1), tick4(5)
    projections(0)
    tick2(1), landed(1), tick0(2), tick3(1), tick1(2), tick4(1)
    for j in range(NCH):
        project(0, j)
    tick2(2), landed(2), tick0(3), tick3(2), tick1(3), tick4(2)
    projections(1)
    tick2(3), landed(3), tick0(4), tick3(3), tick1(4), tick4(3)
    projections(2)
    tick2(4), tick3(4), tick4(4)
    projections(3)
    attend(0)
    attend(1)
    lift((0, 1))
    attend(2)
    lift((2, 3))
    attend(3)
    order = [j for j in range(NCH) if j != LOW] + [LOW]
    for j in order:
        rest(j)
    for j in order:
        finish(j, j == order[0], j == order[-1])

    copies["z", 0, 0].wait_send()
    for j in range(NCH):
        for m in (1, 2, 3):
            copies["z", m, j].wait_send()

        @pl.when(jnp.logical_or(upper == 0, j != LOW))
        def _():
            for t in range(4):
                drain(fwd, fsend, t, j, GR - 1)
                drain(back, bsend, t, j, GR - 1)

        @pl.when(upper == int(j == LOW))
        def _():
            for t in range(2):
                drain(gotx, fxsend, t, j)

        if j != LOW:
            @pl.when(upper == 1)
            def _():
                for t in range(2):
                    drain(homex, bxsend, t, j)

    for p in range(2 + NCH):
        for s in range(1, 17):
            copies[p, s].wait_send()

    @pl.when(upper == 0)
    def _():
        for t in range(4):
            wait(backl.at[t], blsend.at[t])

    @pl.when(upper == 1)
    def _():
        for t in range(2):
            wait(gotl.at[t], flsend.at[t])


def body(inputs, norm_gain, w_qkv, w_out, grad_out):
    vmem, hbm = pl.BlockSpec(memory_space=pltpu.VMEM), pl.BlockSpec(memory_space=pl.ANY)
    four, two = pltpu.VMEM((4, NCH, GR, FG, CH), BF), pltpu.VMEM((2, NCH, GR, FG, CH), BF)
    sem4, sem2 = pltpu.SemaphoreType.DMA((4, NCH)), pltpu.SemaphoreType.DMA((2, NCH))
    outputs, grad_in = pl.pallas_call(
        kernel,
        out_shape=[jax.ShapeDtypeStruct((FR, D), BF)] * 2,
        in_specs=[hbm, vmem, hbm, hbm, hbm],
        out_specs=[vmem] * 2,
        scratch_shapes=[
            pltpu.VMEM((FR, D), BF),
            pltpu.VMEM((FR, D), BF),
            pltpu.VMEM((4, 4, 4, 64, D), BF),
            pltpu.VMEM((FR, D), BF),
            four, four, two, pltpu.VMEM((2, GR, FG, CH), BF), four, two,
            pltpu.VMEM((4, GR, FG, CH), BF), four, two,
            pltpu.VMEM((FR, D), F32),
            pltpu.VMEM((FR, D), F32),
            pltpu.SemaphoreType.DMA((1 + 3 * NCH,)),
            pltpu.SemaphoreType.DMA((1 + 3 * NCH,)),
            pltpu.SemaphoreType.DMA((2 + NCH, 17)),
            pltpu.SemaphoreType.DMA((2 + NCH, 17)),
            pltpu.SemaphoreType.DMA((4,)),
            pltpu.SemaphoreType.DMA((2,)),
            sem4, sem4, sem2, sem2,
            pltpu.SemaphoreType.DMA((2,)),
            pltpu.SemaphoreType.DMA((2,)),
            sem4, sem4, sem2, sem2,
            pltpu.SemaphoreType.DMA((4,)),
        ],
        compiler_params=pltpu.CompilerParams(
            collective_id=0, has_side_effects=True, vmem_limit_bytes=60 * 2**20
        ),
    )(
        inputs.reshape(FR, D),
        norm_gain.reshape(1, D),
        w_qkv.reshape(32, 3 * D),
        w_out.reshape(32, D),
        grad_out.reshape(FR, D),
    )
    return outputs.reshape(FR, 1, D), grad_in.reshape(FR, 1, D)


def solution(mesh):
    return jax.shard_map(
        body,
        mesh=mesh,
        in_specs=(
            P("frame", "cb", None),
            P(),
            P("cb", "frame", None),
            P("cb", "frame", None),
            P("frame", "cb", None),
        ),
        out_specs=(P("frame", "cb", None), P("frame", "cb", None)),
        check_vma=False,
    )
```

```python
import functools

import jax
import jax.numpy as jnp
from jax import lax
from jax.experimental import pallas as pl
from jax.experimental.pallas import tpu as pltpu
from jax.sharding import PartitionSpec as P

D = 1024
CB = 16
FR = 256
GR = 8
FG = FR // GR
CH = 128
NCH = D // CH
GC = 256
NG = D // GC
LOW = 2
EPS = 1e-05
BF = jnp.bfloat16
F32 = jnp.float32
NT = (((1,), (1,)), ((), ()))
NN = (((1,), (0,)), ((), ()))
TN = (((0,), (0,)), ((), ()))


def dot(a, b, dims):
    return lax.dot_general(a, b, dims, preferred_element_type=F32)


def kernel(
    x_hbm, gain_ref, wqkv_ref, wout_ref, g_hbm, out_ref, gin_ref,
    x_ref, g_ref, w, normed, fwd, got, gotx, gotl, back, backx, backl, home, homex, gn, total,
    zsend, zrecv, gsend, grecv, lsem, isem, fsend, frecv, fxsend, fxrecv, flsend, flrecv,
    bsend, brecv, bxsend, bxrecv, blsend,
):
    cb = lax.axis_index("cb")
    fr = lax.axis_index("frame")
    upper, me = cb // GR, cb % GR
    x, y, zh = fr // 8, (fr // 2) % 4, fr % 2
    xr, xl = (x + 1) % 4, (x + 3) % 4
    yr, yl = (y + 1) % 4, (y + 3) % 4

    def at(xx, yy, zz):
        return {"frame": (xx * 4 + yy) * 2 + zz}

    loads = [
        pltpu.make_async_copy(x_hbm, x_ref, isem.at[0]),
        pltpu.make_async_copy(g_hbm, g_ref, isem.at[1]),
    ]
    for load in loads:
        load.start()

    barrier = pltpu.get_barrier_semaphore()
    for peer in (at(x, y, 1 - zh), at(xr, y, zh), at(xl, y, zh), at(x, yr, zh), at(x, yl, zh)):
        pl.semaphore_signal(barrier, inc=1, device_id=peer)

    @pl.loop(1, CB)
    def _(j):
        pl.semaphore_signal(barrier, inc=1, device_id={"cb": (cb + j) % CB})

    ways_x, ways_y = (at(xr, y, zh), at(xl, y, zh)), (at(x, yr, zh), at(x, yl, zh))
    copies = {}

    def keep(m):
        shard = wqkv_ref.at[:, pl.ds((3 - m) * D, D)] if m else wout_ref
        local = pltpu.make_async_copy(shard, w.at[m, x, y, pl.ds(zh * 32, 32), :], lsem.at[m])
        local.start()
        copies[m] = local

    def swap(m, j):
        key = 0 if m == 0 else 1 + 3 * j + m - 1
        width = GC if m else D
        copy = pltpu.make_async_remote_copy(
            src_ref=wqkv_ref.at[:, pl.ds((3 - m) * D + j * GC, GC)] if m else wout_ref,
            dst_ref=w.at[m, x, y, pl.ds(zh * 32, 32), pl.ds(j * GC, width)],
            send_sem=zsend.at[key], recv_sem=zrecv.at[key],
            device_id=at(x, y, 1 - zh), device_id_type=pl.DeviceIdType.MESH,
        )
        copy.start()
        copies["z", m, j] = copy

    def remote(key, src, dst, peer):
        copy = pltpu.make_async_remote_copy(
            src_ref=src, dst_ref=dst, send_sem=gsend.at[key], recv_sem=grecv.at[key],
            device_id=peer, device_id_type=pl.DeviceIdType.MESH,
        )
        copy.start()
        copies[key] = copy

    def view(p, h, xs, ys, half=None):
        if p in (0, 5):
            start = 32 * (zh if p == 0 else 1 - zh)
            rows = pl.ds(start, 32) if half is None else pl.ds(start + 16 * half, 16)
            return w.at[pl.ds(1, 3), xs, ys, rows, pl.ds(h * 128, 128)]
        rows = slice(None) if half is None else pl.ds(32 * half, 32)
        if p == 1:
            return w.at[0, xs, ys, rows, pl.ds(h * 512, 512)]
        return w.at[pl.ds(1, 3), xs, ys, rows, pl.ds((p - 1) * GC + h * 128, 128)]

    def landed(j):
        for m in (1, 2, 3):
            copies["z", m, j].wait_recv()

    def tick0(p):
        for h, ways in ((0, ways_x), (1, ways_y)):
            block = view(p, h, x, y)
            remote((p, 1 + 4 * h), block, block, ways[0])
            remote((p, 2 + 4 * h), block, block, ways[1])

    def tick1(p):
        for h, ways in ((0, ways_x), (1, ways_y)):
            copies[p, 1 + 4 * h].wait_recv()
            block = view(p, h, *((xl, y), (x, yl))[h], 0)
            remote((p, 3 + 4 * h), block, block, ways[0])
        for h, ways in ((0, ways_x), (1, ways_y)):
            copies[p, 2 + 4 * h].wait_recv()
            block = view(p, h, *((xr, y), (x, yr))[h], 1)
            remote((p, 4 + 4 * h), block, block, ways[1])

    def line(p, h, pos, span):
        return view(p, h, *((span, pos), (pos, span))[h])

    def tick2(p):
        for h, ways in ((0, ways_y), (1, ways_x)):
            copies[p, 3 + 4 * h].wait_recv()
            copies[p, 4 + 4 * h].wait_recv()
            block = line(p, h, (y, x)[h], slice(None))
            remote((p, 9 + 4 * h), block, block, ways[0])
            remote((p, 10 + 4 * h), block, block, ways[1])

    def tick3(p):
        for h, ways in ((0, ways_y), (1, ways_x)):
            copies[p, 9 + 4 * h].wait_recv()
            block = line(p, h, (yl, xl)[h], pl.ds(0, 2))
            remote((p, 11 + 4 * h), block, block, ways[0])
        for h, ways in ((0, ways_y), (1, ways_x)):
            copies[p, 10 + 4 * h].wait_recv()
            block = line(p, h, (yr, xr)[h], pl.ds(2, 2))
            remote((p, 12 + 4 * h), block, block, ways[1])

    def tick4(p):
        for s in (11, 12, 15, 16):
            copies[p, s].wait_recv()

    def chunk(j):
        return pl.ds(j * CH, CH)

    def exchange(src, dst, ssem, rsem, t, j, way=None):
        @pl.loop(0, GR)
        def _(i):
            peer = (me + 4 + i) % GR
            wanted = {None: peer != me, 0: peer < me, 1: peer > me}[way]

            @pl.when(wanted)
            def _():
                pltpu.make_async_remote_copy(
                    src_ref=src.at[t, j, peer], dst_ref=dst.at[t, j, me],
                    send_sem=ssem.at[t, j], recv_sem=rsem.at[t, j],
                    device_id={"cb": upper * GR + peer}, device_id_type=pl.DeviceIdType.MESH,
                ).start()

        if way != 1:
            pltpu.make_async_copy(src.at[t, j, me], dst.at[t, j, me], rsem.at[t, j]).start()

    def across(src, dst, ssem, rsem):
        @pl.loop(0, GR)
        def _(i):
            peer = (me + 4 + i) % GR
            pltpu.make_async_remote_copy(
                src_ref=src.at[peer], dst_ref=dst.at[me], send_sem=ssem, recv_sem=rsem,
                device_id={"cb": (1 - upper) * GR + peer}, device_id_type=pl.DeviceIdType.MESH,
            ).start()

    def wait(whole, sem):
        pltpu.make_async_copy(whole, whole, sem).wait()

    def drain(buf, sem, t, j, count=GR):
        wait(buf.at[t, j, pl.ds(0, count)], sem.at[t, j])

    def out_rows(j, part):
        return w[0, j // 2, pl.ds(j % 2 * 2, 2), :, part].reshape(CH, -1)

    def project(m, j):
        if m == 0:
            tile = dot(g_ref[...], out_rows(j, slice(None)), NT)
        else:
            tile = dot(normed[...], w[m, :, :, :, chunk(j)].reshape(D, CH), NN)
        fwd[m, j] = tile.astype(BF).reshape(GR, FG, CH)

        if m in (1, 2):
            @pl.when(upper == int(j == LOW))
            def _():
                across(fwd.at[m, j], gotx.at[m - 1, j], fxsend.at[m - 1, j], fxrecv.at[m - 1, j])
        elif j == LOW:
            @pl.when(upper == 1)
            def _():
                across(fwd.at[m, j], gotl.at[m // 3], flsend.at[m // 3], flrecv.at[m // 3])

        @pl.when(jnp.logical_or(upper == 0, j != LOW))
        def _():
            exchange(fwd, got, fsend, frecv, m, j)

    def projections(g):
        for j in (2 * g, 2 * g + 1):
            for m in (1, 2, 3):
                project(m, j)

    ri = lax.broadcasted_iota(jnp.int32, (FR, FR), 0)
    ci = lax.broadcasted_iota(jnp.int32, (FR, FR), 1)
    low = lax.broadcasted_iota(jnp.int32, (FR, 128), 1) < 64
    zero = jnp.zeros((FR, 128), BF)

    def grads(mine, masks, q, gc, ks, vs):
        q1, gc1 = jnp.where(mine, q, zero), jnp.where(mine, gc, zero)
        scores = [jnp.where(seen, dot(q1, k, NT) * 0.125, -jnp.inf) for seen, k in zip(masks, ks)]
        top = functools.reduce(jnp.maximum, [jnp.max(s, axis=-1, keepdims=True) for s in scores])
        e = [jnp.exp(s - top) for s in scores]
        norm = sum(jnp.sum(s, axis=-1, keepdims=True) for s in e)
        probs = [s / norm for s in e]
        rough = [s.astype(BF) for s in probs]
        gp = [dot(gc1, v, NT) for v in vs]
        inner = sum(jnp.sum(a * b, axis=-1, keepdims=True) for a, b in zip(probs, gp))
        gs = [(a * (b - inner) * 0.125).astype(BF) for a, b in zip(probs, gp)]
        found = [
            sum(dot(a, b, NN) for a, b in zip(gs, ks)),
            dot(gs[0], q, TN),
            dot(rough[0], gc, TN),
            sum(dot(a, b, NN) for a, b in zip(rough, vs)),
        ]
        for a, b in zip(gs[1:], rough[1:]):
            found += [dot(a, q, TN), dot(b, gc, TN)]
        return found

    def heads(j):
        @pl.loop(0, CH // 128)
        def _(i):
            part = pl.ds(pl.multiple_of(i * 128, 128), 128)
            frame = (ri & (FG - 1)) == (ci & (FG - 1))
            causal = jnp.logical_and(frame, ri >= ci)

            def load(*refs):
                return [ref[:, :, part].reshape(FR, 128) for ref in refs]

            def store(refs, results):
                for ref, a, b in zip(refs, *results):
                    ref[:, :, part] = jnp.where(low, a, b).astype(BF).reshape(GR, FG, 128)

            sides = (low, jnp.logical_not(low))
            backs = [back.at[t, j] for t in range(4)]

            def apart(extra):
                gc, v, k, q = load(*(got.at[t, j] for t in range(4)))
                vs, ks, masks = [v], [k], [causal]
                if extra:
                    vx, kx = load(gotx.at[0, j], gotx.at[1, j])
                    vs, ks, masks = [v, vx], [k, kx], [causal, frame]
                store(
                    backs + [backx.at[0, j], backx.at[1, j]] * extra,
                    [grads(mine, masks, q, gc, ks, vs) for mine in sides],
                )

            def together():
                gc, v, k, q = load(*(got.at[t, j] for t in range(4)))
                vh, kh, gch, qh = load(gotx.at[0, j], gotx.at[1, j], gotl.at[0], gotl.at[1])
                results = []
                for mine in sides:
                    a = grads(mine, [causal], q, gc, [k], [v])
                    b = grads(mine, [causal, frame], qh, gch, [kh, k], [vh, v])
                    results.append([a[0], a[1] + b[4], a[2] + b[5], a[3]] + b[:4])
                store(backs + [backl.at[t] for t in range(4)], results)

            pl.when(j == LOW)(together)
            pl.when(jnp.logical_and(j != LOW, upper == 0))(lambda: apart(0))
            pl.when(jnp.logical_and(j != LOW, upper == 1))(lambda: apart(1))

    def attend(j):
        @pl.when(jnp.logical_or(upper == 0, j != LOW))
        def _():
            for t in range(4):
                drain(got, frecv, t, j)

            @pl.when(jnp.logical_or(upper == 1, j == LOW))
            def _():
                for t in range(2):
                    drain(gotx, fxrecv, t, j)

            @pl.when(j == LOW)
            def _():
                for t in range(2):
                    wait(gotl.at[t], flrecv.at[t])

            heads(j)

            @pl.when(upper == 1)
            def _():
                for t in range(2):
                    across(backx.at[t, j], homex.at[t, j], bxsend.at[t, j], bxrecv.at[t, j])

            for t in range(4):
                exchange(back, home, bsend, brecv, t, j, 0)

    def rest(j):
        @pl.when(jnp.logical_or(upper == 0, j != LOW))
        def _():
            for t in range(4):
                exchange(back, home, bsend, brecv, t, j, 1)

    def lift(ts):
        @pl.when(upper == 0)
        def _():
            for t in ts:
                across(backl.at[t], home.at[t, LOW], blsend.at[t], brecv.at[t, LOW])

    def finish(j, first=False, last=False):
        for t in range(3):
            drain(home, brecv, t, j)

        @pl.when(jnp.logical_and(upper == 0, j != LOW))
        def _():
            for t in range(2):
                drain(homex, bxrecv, t, j)
                home[t + 1, j] = (home[t + 1, j].astype(F32) + homex[t, j].astype(F32)).astype(BF)

        @pl.loop(0, 4)
        def _(i):
            part = pl.ds(pl.multiple_of(i * 256, 256), 256)
            tile = sum(
                dot(home[t, j].reshape(FR, CH), w[3 - t, i, :, :, chunk(j)].reshape(256, CH), NT)
                for t in range(3)
            )
            gn[:, part] = tile if first else gn[:, part] + tile

        if last:
            @pl.loop(0, 8)
            def _(i):
                rows = pl.ds(pl.multiple_of(i * 32, 32), 32)
                wide = x_ref[rows, :].astype(F32)
                r = lax.rsqrt(jnp.mean(wide * wide, axis=-1, keepdims=True) + EPS)
                s = gn[rows, :] * gain_ref[...]
                inner = jnp.mean(s * wide, axis=-1, keepdims=True)
                gin_ref[rows, :] = (
                    g_ref[rows, :].astype(F32) + r * (s - wide * (r * r * inner))
                ).astype(BF)

        drain(home, brecv, 3, j)

        @pl.loop(0, 4)
        def _(i):
            part = pl.ds(pl.multiple_of(i * 256, 256), 256)
            tile = dot(
                home[3, j].reshape(FR, CH), out_rows(j, part), NN
            )
            tile = tile + (x_ref[:, part].astype(F32) if first else total[:, part])
            if last:
                out_ref[:, part] = tile.astype(BF)
            else:
                total[:, part] = tile

    for m in (1, 2, 3, 0):
        keep(m)

    loads[0].wait()

    @pl.loop(0, 8)
    def _(i):
        rows = pl.ds(pl.multiple_of(i * 32, 32), 32)
        wide = x_ref[rows, :].astype(F32)
        r = lax.rsqrt(jnp.mean(wide * wide, axis=-1, keepdims=True) + EPS)
        normed[rows, :] = (wide * r * gain_ref[...]).astype(BF)

    for m in (1, 2, 3):
        copies[m].wait()
    pl.semaphore_wait(barrier, 5 + CB - 1)

    for m in (1, 2, 3):
        swap(m, 0)
    tick0(0)
    swap(0, 0)
    tick1(0)
    landed(0)
    tick0(5), tick2(0), tick1(5), tick3(0), tick2(5)
    for j in range(1, NG):
        for m in (1, 2, 3):
            swap(m, j)
    loads[1].wait()
    copies[0].wait()
    copies["z", 0, 0].wait_recv()
    tick0(1), tick4(0), tick3(5), tick1(1), tick4(5)
    projections(0)
    tick2(1), landed(1), tick0(2), tick3(1), tick1(2), tick4(1)
    for j in range(NCH):
        project(0, j)
    tick2(2), landed(2), tick0(3), tick3(2), tick1(3), tick4(2)
    projections(1)
    tick2(3), landed(3), tick0(4), tick3(3), tick1(4), tick4(3)
    projections(2)
    tick2(4), tick3(4), tick4(4)
    projections(3)
    @pl.loop(0, NCH)
    def _(j):
        attend(j)
        pl.when(j == LOW)(lambda: lift((0, 1)))
        pl.when(j == LOW + 1)(lambda: lift((2, 3)))

    for j in range(NCH):
        rest(j)
    for j in range(NCH):
        finish(j, j == 0, j == NCH - 1)

    copies["z", 0, 0].wait_send()
    for j in range(NG):
        for m in (1, 2, 3):
            copies["z", m, j].wait_send()

    for j in range(NCH):
        @pl.when(jnp.logical_or(upper == 0, j != LOW))
        def _():
            for t in range(4):
                drain(fwd, fsend, t, j, GR - 1)
                drain(back, bsend, t, j, GR - 1)

        @pl.when(upper == int(j == LOW))
        def _():
            for t in range(2):
                drain(gotx, fxsend, t, j)

        if j != LOW:
            @pl.when(upper == 1)
            def _():
                for t in range(2):
                    drain(homex, bxsend, t, j)

    for p in range(2 + NG):
        for s in range(1, 17):
            copies[p, s].wait_send()

    @pl.when(upper == 0)
    def _():
        for t in range(4):
            wait(backl.at[t], blsend.at[t])

    @pl.when(upper == 1)
    def _():
        for t in range(2):
            wait(gotl.at[t], flsend.at[t])


def body(inputs, norm_gain, w_qkv, w_out, grad_out):
    vmem, hbm = pl.BlockSpec(memory_space=pltpu.VMEM), pl.BlockSpec(memory_space=pl.ANY)
    four, two = pltpu.VMEM((4, NCH, GR, FG, CH), BF), pltpu.VMEM((2, NCH, GR, FG, CH), BF)
    sem4, sem2 = pltpu.SemaphoreType.DMA((4, NCH)), pltpu.SemaphoreType.DMA((2, NCH))
    outputs, grad_in = pl.pallas_call(
        kernel,
        out_shape=[jax.ShapeDtypeStruct((FR, D), BF)] * 2,
        in_specs=[hbm, vmem, hbm, hbm, hbm],
        out_specs=[vmem] * 2,
        scratch_shapes=[
            pltpu.VMEM((FR, D), BF),
            pltpu.VMEM((FR, D), BF),
            pltpu.VMEM((4, 4, 4, 64, D), BF),
            pltpu.VMEM((FR, D), BF),
            four, four, two, pltpu.VMEM((2, GR, FG, CH), BF), four, two,
            pltpu.VMEM((4, GR, FG, CH), BF), four, two,
            pltpu.VMEM((FR, D), F32),
            pltpu.VMEM((FR, D), F32),
            pltpu.SemaphoreType.DMA((1 + 3 * NG,)),
            pltpu.SemaphoreType.DMA((1 + 3 * NG,)),
            pltpu.SemaphoreType.DMA((2 + NG, 17)),
            pltpu.SemaphoreType.DMA((2 + NG, 17)),
            pltpu.SemaphoreType.DMA((4,)),
            pltpu.SemaphoreType.DMA((2,)),
            sem4, sem4, sem2, sem2,
            pltpu.SemaphoreType.DMA((2,)),
            pltpu.SemaphoreType.DMA((2,)),
            sem4, sem4, sem2, sem2,
            pltpu.SemaphoreType.DMA((4,)),
        ],
        compiler_params=pltpu.CompilerParams(
            collective_id=0, has_side_effects=True, vmem_limit_bytes=60 * 2**20
        ),
    )(
        inputs.reshape(FR, D),
        norm_gain.reshape(1, D),
        w_qkv.reshape(32, 3 * D),
        w_out.reshape(32, D),
        grad_out.reshape(FR, D),
    )
    return outputs.reshape(FR, 1, D), grad_in.reshape(FR, 1, D)


def solution(mesh):
    return jax.shard_map(
        body,
        mesh=mesh,
        in_specs=(
            P("frame", "cb", None),
            P(),
            P("cb", "frame", None),
            P("cb", "frame", None),
            P("frame", "cb", None),
        ),
        out_specs=(P("frame", "cb", None), P("frame", "cb", None)),
        check_vma=False,
    )
```
